128 devices in a mesh: ctx: 64 (over z, y, x), head: 2 (over core).
Axes of the slice: x: 4, y: 4, z: 4, core: 2. Of those that a mesh axis runs over, the one named last changes fastest.
Arguments:
- ssm_input: bfloat16 [16384, 4096], P('ctx', 'head'), may hold values from -6 to 6
- gate_input: bfloat16 [16384, 4096], P('ctx', 'head'), may hold values from -6 to 6
- b_input: bfloat16 [16384, 512], P('ctx', 'head'), may hold values from -0.375 to 0.375
- c_input: bfloat16 [16384, 512], P('ctx', 'head'), may hold values from -0.375 to 0.375
- step_size: float32 [16384, 64], P('ctx', 'head'), may hold values from 0.25 to 1
- decay_log: float32 [16384, 64], P('ctx', 'head'), may hold values from -0.8 to 0
- skip_gain: float32 [64], P('head'), may hold values from 0.1 to 1.9
- norm_gain: float32 [4096], P('head'), may hold values from 0.5 to 1.5
- queries: bfloat16 [16384, 8192], P('ctx', 'head'), may hold values from -240 to 240
- key_rows: bfloat16 [16384, 1024], P('ctx', 'head'), may hold values from -6 to 6
- value_rows: bfloat16 [16384, 1024], P('ctx', 'head'), may hold values from -6 to 6
- doc_lengths: int32 [32], replicated, may hold values from 1 to 1024, 16384 in all
Outputs:
- ssm_out: bfloat16 [16384, 4096], P('ctx', 'head')
- attn_out: bfloat16 [16384, 8192], P('ctx', 'head')
The draws below stay inside these ranges and needn't reach their ends.
Inputs may be any that keep to these rules, and one draw needn't show every extreme that they name: `doc_lengths`: the 32 documents lie end to end and fill all 16384 tokens; the longest has exactly 1024 tokens.
All inputs are finite; a program needn't handle non-finite values.
Results may differ from the reference program's by a relative error of at most 0.005.
Values may be sent and summed in bfloat16 or wider, within the bound.
A program may use at most 256 MiB of HBM per device.

```python
import math
import jax
import jax.numpy as jnp
import numpy as np
from jax import lax

SSM_HEADS = 64
HEAD_P = 64
STATE = 128
GROUPS = 4
Q_HEADS = 64
KV_HEADS = 8
HEAD_DIM = 128
STRETCH = 128
SPAN = 4
TOK_DEV = 256
SLAB_TOKENS = 16384
LONGEST_DOCUMENT = 1024
DOCS = 32
N_CTX = 64


def draw_decay_log(key, part):
    key_matrix = jax.random.split(key, 6)
    slow_share = 0.5
    slow = jax.random.uniform(key_matrix[0], (SSM_HEADS,)) < slow_share
    slow_rate = jnp.exp(jax.random.uniform(key_matrix[1], (SSM_HEADS,), minval=math.log(0.02), maxval=math.log(0.6))) / LONGEST_DOCUMENT
    fast_rate = jnp.exp(jax.random.uniform(key_matrix[2], (SSM_HEADS,), minval=math.log(1.0 / 50.0), maxval=math.log(1.0 / 25.0)))
    decay_speed = jnp.where(slow, slow_rate, fast_rate)
    coarse_estimate = jnp.exp(jax.random.uniform(key_matrix[3], (SLAB_TOKENS, SSM_HEADS), minval=math.log(0.5), maxval=math.log(2.0)))
    sudden_spike = jax.random.uniform(key_matrix[4], (SLAB_TOKENS, 1)) < 2.0 / LONGEST_DOCUMENT
    training_loss = jax.random.uniform(key_matrix[5], (SLAB_TOKENS, SSM_HEADS), minval=0.22, maxval=0.69)
    return (-(decay_speed[None, :] * coarse_estimate) - jnp.where(sudden_spike, training_loss, 0.0)).astype(jnp.float32)


def draw_queries(key, part):
    key_matrix = jax.random.split(key, 1)
    base = jnp.clip(jax.random.normal(key_matrix[0], (SLAB_TOKENS, Q_HEADS, HEAD_DIM), jnp.float32), -6.0, 6.0)
    return base.reshape(SLAB_TOKENS, Q_HEADS * HEAD_DIM).astype(jnp.bfloat16)


def level_of(rng, dims, shards, low, high):
    def one(position, parts):
        steps = jax.random.uniform(jax.random.fold_in(jax.random.fold_in(rng, 6), position), (parts,), jnp.float32, low / len(shards), high / len(shards))
        return jnp.repeat(jnp.exp(steps), dims[position] // parts).reshape((-1,) + (1,) * (len(dims) - position - 1))

    loudness = one(*shards[0])
    for cut in shards[1:]:
        loudness = loudness * one(*cut)
    return loudness


def split_up(amount, total, reach, slope):
    loads = [(1 << 20) // math.isqrt(standing ** slope) + 1 for standing in range(2, amount + 1)]
    surplus, counts = total - reach - (amount - 1), [1] * (amount - 1)
    while surplus > 0:
        free = [i for i in range(amount - 1) if counts[i] < reach]
        mass, left = sum([loads[i] for i in free]), surplus
        for i in free:
            addition = min(reach - counts[i], max(1, left * loads[i] // mass), surplus)
            counts[i] = counts[i] + addition
            surplus = surplus - addition
    return np.array([reach] + counts)


def uneven_parts(stream_key, count, total, bound, skew):
    if count == 2:
        one = jax.random.randint(stream_key, (), max(1, total - bound), min(bound, total - 1) + 1)
        return jnp.stack([one, total - one])
    tallies = jnp.asarray(split_up(count, total, bound, skew), jnp.int32)
    couples = (count - 1) // 2
    source_of, receiver = tallies[1:1 + 2 * couples:2], tallies[2:2 + 2 * couples:2]
    margin = jnp.minimum(source_of - 1, bound - receiver)
    moved = jax.random.randint(jax.random.fold_in(stream_key, 1), (couples,), 0, 1 << 20) % (margin + 1)
    tallies = tallies.at[1:1 + 2 * couples:2].set(source_of - moved).at[2:2 + 2 * couples:2].set(receiver + moved)
    return tallies[jax.random.permutation(jax.random.fold_in(stream_key, 2), count)]


def scatter_about(stream_key, shape, scale, most, cuts=(), kind=jnp.bfloat16):
    values = scale * jax.random.normal(stream_key, shape, jnp.float32)
    if cuts:
        values = values * level_of(stream_key, shape, cuts, -0.22, 0.18)
    return jnp.clip(values, -most, most).astype(kind)


def setup_inputs(seed: int = 0) -> dict:
    seeds = jax.random.split(jax.random.key(seed), 13)
    ssm_input = scatter_about(seeds[0], (SLAB_TOKENS, SSM_HEADS * HEAD_P), 1.0, 6.0, ((0, 64), (1, 2)))
    gate_input = scatter_about(seeds[1], (SLAB_TOKENS, SSM_HEADS * HEAD_P), 1.0, 6.0, ((0, 64), (1, 2)))
    b_input = scatter_about(seeds[2], (SLAB_TOKENS, GROUPS * STATE), 0.06, 0.375, ((0, 64), (1, 2)))
    c_input = scatter_about(seeds[3], (SLAB_TOKENS, GROUPS * STATE), 0.06, 0.375, ((0, 64), (1, 2)))
    step_size = jnp.clip(jnp.exp(math.log(1.0) - 1.3862944 * jax.random.uniform(seeds[4], (SLAB_TOKENS, SSM_HEADS), jnp.float32) ** level_of(seeds[4], (SLAB_TOKENS, SSM_HEADS), ((0, 64), (1, 2)), -0.2, 0.2)), 0.25, 1.0)
    decay_log = draw_decay_log(jax.random.fold_in(seeds[12], 71), 0)
    skip_gain = jnp.clip(1.0 + 0.18 * jax.random.normal(seeds[6], (SSM_HEADS,), jnp.float32), 0.1, 1.9)
    norm_gain = jnp.clip(1.0 + 0.1 * jax.random.normal(seeds[7], (SSM_HEADS * HEAD_P,), jnp.float32), 0.5, 1.5)
    queries = draw_queries(jax.random.fold_in(seeds[12], 71), 0)
    key_rows = scatter_about(seeds[9], (SLAB_TOKENS, KV_HEADS * HEAD_DIM), 1.0, 6.0, ((0, 64), (1, 2)))
    value_rows = scatter_about(seeds[10], (SLAB_TOKENS, KV_HEADS * HEAD_DIM), 1.0, 6.0, ((0, 64), (1, 2)))
    doc_lengths = uneven_parts(seeds[11], DOCS, SLAB_TOKENS, LONGEST_DOCUMENT, 2).astype(jnp.int32)
    return {"ssm_input": ssm_input, "gate_input": gate_input, "b_input": b_input, "c_input": c_input, "step_size": step_size, "decay_log": decay_log, "skip_gain": skip_gain, "norm_gain": norm_gain, "queries": queries, "key_rows": key_rows, "value_rows": value_rows, "doc_lengths": doc_lengths}


epsilon = 1e-05

def doc_index(doc_lengths, positions):
    ends = jnp.cumsum(doc_lengths, dtype=jnp.int32)
    return lax.optimization_barrier(jnp.sum((ends[None, :] <= positions[:, None]).astype(jnp.int32), axis=1))

def block_terms(ssm_block, b_block, c_block, step_block, decay_block, doc_block, doc_before, group_count):
    length = ssm_block.shape[0]
    head_count = step_block.shape[1]
    share_count = head_count // group_count
    cum_decay = jnp.cumsum(decay_block, axis=0)
    order_ids = jnp.arange(length, dtype=jnp.int32)
    same_doc = (doc_block[:, None] == doc_block[None, :]) & (order_ids[:, None] >= order_ids[None, :])
    cum_rows = cum_decay.T
    spread = cum_rows[:, :, None] - cum_rows[:, None, :]
    decay_mask = jnp.where(same_doc[None], jnp.exp(jnp.where(same_doc[None], spread, 0.0)), 0.0)
    b_groups = b_block.reshape(length, group_count, STATE)
    c_groups = c_block.reshape(length, group_count, STATE)
    scores = jnp.einsum('ign,jgn->gij', c_groups.astype(jnp.float32), b_groups.astype(jnp.float32))
    weights = (scores[:, None] * decay_mask.reshape(group_count, share_count, length, length) * step_block.T.reshape(group_count, share_count, 1, length)).astype(jnp.bfloat16)
    weights = lax.optimization_barrier(weights).astype(jnp.float32)
    ssm_groups = ssm_block.reshape(length, group_count, share_count, HEAD_P)
    intra_out = jnp.einsum('grij,jgrp->igrp', weights, ssm_groups.astype(jnp.float32))
    last_doc = (doc_block == doc_block[-1]).astype(jnp.float32)
    ending = jnp.exp(cum_decay[-1][None, :] - cum_decay) * last_doc[:, None] * step_block
    scaled = (ssm_groups.astype(jnp.float32) * ending.reshape(length, group_count, share_count, 1)).astype(jnp.bfloat16)
    scaled = lax.optimization_barrier(scaled).astype(jnp.float32)
    block_state = jnp.einsum('jgrp,jgn->grpn', scaled, b_groups.astype(jnp.float32)).reshape(head_count, HEAD_P, STATE)
    joined = (doc_block[-1] == doc_before).astype(jnp.float32)
    carry_gain = jnp.exp(cum_decay[-1]) * joined
    read_gain = jnp.exp(cum_decay) * (doc_block == doc_before).astype(jnp.float32)[:, None]
    return (intra_out.reshape(length, head_count * HEAD_P), block_state, carry_gain, read_gain)

def state_read(c_block, entering, read_gain, group_count):
    length = c_block.shape[0]
    head_count = read_gain.shape[1]
    share_count = head_count // group_count
    c_groups = c_block.reshape(length, group_count, STATE).astype(jnp.float32)
    result = jnp.einsum('ign,grpn->igrp', c_groups, entering.reshape(group_count, share_count, HEAD_P, STATE), precision=lax.Precision.HIGHEST)
    return (result * read_gain.reshape(length, group_count, share_count, 1)).reshape(length, head_count * HEAD_P)

def reference(ssm_input, gate_input, b_input, c_input, step_size, decay_log, skip_gain, norm_gain, queries, key_rows, value_rows, doc_lengths):
    block_count = SLAB_TOKENS // STRETCH
    positions = jnp.arange(SLAB_TOKENS, dtype=jnp.int32)
    doc_ids = doc_index(doc_lengths, positions)
    doc_before = doc_index(doc_lengths, jnp.arange(block_count, dtype=jnp.int32) * STRETCH - 1)
    skip_rows = jnp.repeat(skip_gain, HEAD_P)

    def per_block(entering, inputs):
        ssm_block, gate_block, b_block, c_block, step_block, decay_block, doc_block, before_one = inputs
        intra_out, block_state, carry_gain, read_gain = block_terms(ssm_block, b_block, c_block, step_block, decay_block, doc_block, before_one, GROUPS)
        ssm_y = intra_out + state_read(c_block, entering, read_gain, GROUPS) + skip_rows[None, :] * ssm_block.astype(jnp.float32)
        gated = ssm_y * jax.nn.silu(gate_block.astype(jnp.float32))
        mean_square = lax.optimization_barrier(jnp.mean(gated * gated, axis=1))
        result = (gated * lax.rsqrt(mean_square + epsilon)[:, None] * norm_gain[None, :]).astype(jnp.bfloat16)
        return (carry_gain[:, None, None] * entering + block_state, result)
    stacked = (ssm_input.reshape(block_count, STRETCH, -1), gate_input.reshape(block_count, STRETCH, -1), b_input.reshape(block_count, STRETCH, -1), c_input.reshape(block_count, STRETCH, -1), step_size.reshape(block_count, STRETCH, -1), decay_log.reshape(block_count, STRETCH, -1), doc_ids.reshape(block_count, STRETCH), doc_before)
    initial = jnp.zeros((SSM_HEADS, HEAD_P, STATE), jnp.float32)
    final_state, ssm_blocks = lax.scan(per_block, initial, stacked)
    ssm_out = ssm_blocks.reshape(SLAB_TOKENS, SSM_HEADS * HEAD_P)
    share_q = Q_HEADS // KV_HEADS
    query_heads = queries.reshape(SLAB_TOKENS, KV_HEADS, share_q, HEAD_DIM)
    window = (SPAN + 1) * TOK_DEV
    score_scale = 1.0 / math.sqrt(HEAD_DIM)

    def per_shard(shard):
        start = (shard * TOK_DEV).astype(jnp.int32)
        key_start = jnp.maximum(start - SPAN * TOK_DEV, 0).astype(jnp.int32)
        query_block = lax.dynamic_slice_in_dim(query_heads, start, TOK_DEV, 0).astype(jnp.float32)
        key_block = lax.dynamic_slice_in_dim(key_rows, key_start, window, 0).reshape(window, KV_HEADS, HEAD_DIM).astype(jnp.float32)
        value_block = lax.dynamic_slice_in_dim(value_rows, key_start, window, 0).reshape(window, KV_HEADS, HEAD_DIM).astype(jnp.float32)
        query_pos = start + jnp.arange(TOK_DEV, dtype=jnp.int32)
        key_pos = key_start + jnp.arange(window, dtype=jnp.int32)
        query_docs = doc_index(doc_lengths, query_pos)
        key_docs = doc_index(doc_lengths, key_pos)
        allowed = (key_docs[None, :] == query_docs[:, None]) & (key_pos[None, :] <= query_pos[:, None])
        logits = jnp.einsum('tkre,wke->tkrw', query_block, key_block) * score_scale
        logits = jnp.where(allowed[:, None, None, :], logits, -jnp.inf)
        peak = lax.optimization_barrier(jnp.max(logits, axis=3))
        raw = jnp.exp(logits - peak[..., None])
        denom = lax.optimization_barrier(jnp.sum(raw, axis=3))
        probs = lax.optimization_barrier(raw.astype(jnp.bfloat16)).astype(jnp.float32)
        result = jnp.einsum('tkrw,wke->tkre', probs, value_block) / denom[..., None]
        return result.reshape(TOK_DEV, Q_HEADS * HEAD_DIM).astype(jnp.bfloat16)
    attn_out = lax.map(per_shard, jnp.arange(N_CTX, dtype=jnp.int32)).reshape(SLAB_TOKENS, Q_HEADS * HEAD_DIM)
    return (ssm_out, attn_out)
```

```python
import math

import jax
import jax.numpy as jnp
from jax import lax
from jax.experimental import pallas as pl
from jax.experimental.pallas import tpu as pltpu
from jax.sharding import PartitionSpec as P

ROWS = 256
BLK = 128
HP = 64
PAIRS = 16
LANES = 2048
EPS = 1e-05
CHANNELS = 4096
FAR = 2**30
SCALE = 1.0 / math.sqrt(128.0)
F32 = jnp.float32
BF16 = jnp.bfloat16
HIGH = lax.Precision.HIGHEST
MESH = pl.DeviceIdType.MESH
NT = (((1,), (1,)), ((), ()))
KV, ST, CR = 0, 1, 2
ORDER = ((KV, 0), (KV, 1), (CR, 0), (ST, 0), (ST, 1), (KV, 2), (KV, 3), (ST, 2), (ST, 3))
LEFT = ((KV, 0), (KV, 1), (ST, 0), (ST, 1))


def dot(a, b, precision=None):
    return jnp.dot(a, b, preferred_element_type=F32, precision=precision)


def dot_nt(a, b):
    return lax.dot_general(a, b, NT, preferred_element_type=F32)


def split3(v):
    hi = v.astype(BF16)
    rest = v - hi.astype(F32)
    mid = rest.astype(BF16)
    return hi, mid, (rest - mid.astype(F32)).astype(BF16)


def body(
    doc_ref, x_ref, b_ref, c_ref, step_ref, decay_ref, skip_ref, gain_ref, k_ref, v_ref, z_hbm, q_hbm,
    ssm_out, attn_out,
    z_ref, q_ref, kbuf, vbuf, tbuf, cbuf, town, cown, qaug, kaug, acc, peak,
    dpad, spad, cum_s, cum3, cum_t, step_t, end_t, scm, bt, intra, rgain, spread, bs0, enter0, enter1,
    sq_own, sq_other,
    lsem, kvs, kvr, sts, str_, qsem,
):
    d = lax.axis_index("ctx")
    head = lax.axis_index("head")
    n = lax.axis_size("ctx")
    x = lax.rem(d, 4)

    def at(off):
        return {"ctx": lax.rem(d + off + n, n)}

    right = {"ctx": jnp.where(x == 3, d - 3, d + 1)}
    left = {"ctx": jnp.where(x == 0, d + 3, d - 1)}
    other = {"head": 1 - head}
    z_copy = pltpu.make_async_copy(z_hbm, z_ref, lsem.at[0])
    q_copy = pltpu.make_async_copy(q_hbm, q_ref, lsem.at[1])
    q_copy.start()
    z_copy.start()
    barrier = pltpu.get_barrier_semaphore()
    for peer in (at(4), at(-4), at(1), at(-1), right, left, other):
        pl.semaphore_signal(barrier, inc=1, device_id=peer, device_id_type=MESH)
    pl.semaphore_wait(barrier, 7)

    def send(item, src, dist, to):
        kind, i = item
        s, r = dist - 1, dist - 1
        if kind == KV:
            lanes = pl.ds(i * 128, 128)
            pairs = ((k_ref, kbuf, 0), (v_ref, vbuf, 1))
            return [
                pltpu.make_async_remote_copy(
                    own.at[:, lanes] if src == 0 else buf.at[src - 1, :, lanes],
                    buf.at[dist - 1, :, lanes],
                    kvs.at[s, i, j], kvr.at[r, i, j], device_id=to, device_id_type=MESH,
                )
                for own, buf, j in pairs
            ]
        if kind == ST:
            lanes = pl.ds(i * 512, 512)
            return [
                pltpu.make_async_remote_copy(
                    town.at[:, lanes] if src == 0 else tbuf.at[src - 1, :, lanes],
                    tbuf.at[dist - 1, :, lanes],
                    sts.at[s, i], str_.at[r, i], device_id=to, device_id_type=MESH,
                )
            ]
        return [
            pltpu.make_async_remote_copy(
                cown if src == 0 else cbuf.at[src - 1], cbuf.at[dist - 1],
                sts.at[s, 4], str_.at[r, 4], device_id=to, device_id_type=MESH,
            )
        ]

    def start(copies):
        for copy in copies:
            copy.start()

    def arrive(item, dist):
        for copy in send(item, 0, dist, at(4)):
            copy.wait_recv()

    def send_own(items):
        for item in items:
            start(send(item, 0, 4, at(4)))

        @pl.when(x < 3)
        def _():
            for item in items:
                start(send(item, 0, 1, right))

        @pl.when(x == 0)
        def _():
            for item in items:
                start(send(item, 0, 3, left))

    def got4(item):
        arrive(item, 4)

        @pl.when(x > 0)
        def _():
            start(send(item, 4, 3, left))

        @pl.when(x == 3)
        def _():
            start(send(item, 4, 1, right))

    def got1(item):
        arrive(item, 1)
        if item not in LEFT:
            start(send(item, 1, 2, at(1)))

    def got3(item):
        arrive(item, 3)
        if item in LEFT:
            start(send(item, 3, 2, at(-1)))

    def got2(item):
        arrive(item, 2)

    send_own(ORDER[:2])

    lane = lax.broadcasted_iota(jnp.int32, (1, 128), 1)

    def one_doc(j, carry):
        run, first, last = carry
        length = doc_ref[j]
        first = jnp.where(lane == j, run, first)
        last = jnp.where(lane == j, run + length, last)
        return run + length, first, last

    first0 = jnp.where(lane == 127, -FAR, FAR)
    last0 = jnp.where(lane == 127, 0, -FAR)
    _, first, last = lax.fori_loop(0, 32, one_doc, (jnp.int32(0), first0, last0))

    def marks(base, rows):
        pos = base + lax.broadcasted_iota(jnp.int32, (rows, 128), 0)
        return jnp.where((pos >= first) & (pos < last), 1.0, 0.0).astype(F32)

    row0 = d * ROWS
    own_marks = marks(row0, ROWS)
    qaug[...] = ((own_marks - 1.0) * float(FAR)).astype(BF16)
    for j in range(5):
        kaug[j] = (own_marks if j == 0 else marks(row0 - j * ROWS, ROWS)).astype(BF16)

    dpad[...] = jnp.zeros_like(dpad)
    spad[...] = jnp.zeros_like(spad)
    dpad[:, 0:32] = decay_ref[...]
    spad[:, 0:32] = step_ref[...]
    ti = lax.broadcasted_iota(jnp.int32, (BLK, BLK), 0)
    si = lax.broadcasted_iota(jnp.int32, (BLK, BLK), 1)
    causal = ti >= si
    tri = causal.astype(F32)
    shift = [
        ((si == ti + 32 * k) & (ti < 32)).astype(BF16) for k in range(3)
    ]
    spread_i = lax.broadcasted_iota(jnp.int32, (BLK, LANES), 0)
    spread_l = lax.broadcasted_iota(jnp.int32, (BLK, LANES), 1)
    spread[...] = jnp.where(lax.shift_right_logical(spread_l, 6) == spread_i, 1.0, 0.0)
    carry_total = jnp.where(lane < 32, 1.0, 0.0)
    carry_rows = []
    for i in range(2):
        rows = slice(i * BLK, (i + 1) * BLK)
        oh = own_marks[rows]
        before = marks(row0 + i * BLK - 1, 8)[0:1]
        oh_last = oh[BLK - 1 : BLK]
        cum = dot(tri, dpad[rows], HIGH)
        cum_s[rows] = cum
        ct = cum.T
        cum_t[i] = ct
        stt = spad[rows].T
        step_t[i] = stt
        ohb = oh.astype(BF16)
        same = dot_nt(ohb, ohb)
        allowed = causal & (same > 0.5)
        last_row = same[BLK - 1 : BLK]
        end_t[i] = jnp.exp(ct[:, BLK - 1 : BLK] - ct) * last_row * stt
        for g in range(2):
            cols = slice(g * 128, (g + 1) * 128)
            sc = dot_nt(c_ref[rows, cols], b_ref[rows, cols])
            scm[2 * i + g] = jnp.where(allowed, sc, 0.0)
            bt[2 * i + g] = b_ref[rows, cols].astype(F32).T
        hi, mid, lo = split3(cum)
        cum3[rows] = (dot(hi, shift[0]) + dot(mid, shift[1]) + dot(lo, shift[2])).astype(BF16)
        joined = jnp.sum(oh_last * before, axis=1, keepdims=True)
        gain_row = jnp.where(lane < 32, jnp.exp(cum[BLK - 1 : BLK]) * joined, 0.0)
        carry_rows.append(gain_row)
        carry_total = carry_total * gain_row
        reads = jnp.sum(oh * before, axis=1, keepdims=True)
        rg = jnp.exp(cum) * reads
        rhi = rg.astype(BF16)
        rlo = (rg - rhi.astype(F32)).astype(BF16)
        e16 = spread[...].astype(BF16)
        rgain[rows] = dot(rhi, e16) + dot(rlo, e16)
    cown[...] = jnp.broadcast_to(carry_total, (8, 128))
    row_id = lax.broadcasted_iota(jnp.int32, (8, 128), 0)
    skip_pad = jnp.broadcast_to(skip_ref[...], (8, 128))
    small = jnp.where(row_id == 0, carry_rows[0], jnp.where(row_id == 1, carry_rows[1], skip_pad))
    wide = dot(small, spread[...], HIGH)
    carry0_w, carry1_w, skip_w = wide[0:1], wide[1:2], wide[2:3]
    spad[0:8] = small
    start_lane = lax.broadcasted_iota(jnp.int32, (BLK, 256), 1)
    start_row = lax.broadcasted_iota(jnp.int32, (BLK, 256), 0)
    low = lax.broadcasted_iota(jnp.int32, (BLK, BLK), 1) < HP
    enter0[0:8] = wide

    def pair(p, _):
        lanes = pl.ds(pl.multiple_of(p * 128, 128), 128)
        pick = jnp.where(
            ((start_row & 31) == 2 * p + lax.shift_right_logical(start_lane, 7)) & (start_row < 96), 1.0, 0.0
        ).astype(BF16)
        cols = dot(cum3[...], pick)
        g = lax.shift_right_logical(p, 3)
        outs = []
        for i in range(2):
            xs = x_ref[i * BLK : (i + 1) * BLK, lanes]
            parts = []
            sg = scm[2 * i + g]
            bg = bt[2 * i + g]
            for e in range(2):
                crow = cum_t[i, pl.ds(2 * p + e, 1), :]
                srow = step_t[i, pl.ds(2 * p + e, 1), :]
                diff = jnp.minimum(cols[i * BLK : (i + 1) * BLK, e * 128 : (e + 1) * 128] - crow, 0.0)
                parts.append((sg * jnp.exp(diff) * srow).astype(BF16))
            for e in range(2):
                erow = end_t[i, pl.ds(2 * p + e, 1), :]
                parts.append((bg * erow).astype(BF16))
            res = dot(jnp.concatenate(parts, axis=0), xs)
            intra[i * BLK : (i + 1) * BLK, lanes] = jnp.where(low, res[0:128], res[128:256])
            outs.append(jnp.where(low, res[256:384], res[384:512]))
        bs0[:, lanes] = outs[0]
        c1 = enter0[1:2, lanes]
        town[:, lanes] = (c1 * outs[0] + outs[1]).astype(BF16)
        return 0

    lax.fori_loop(0, PAIRS, pair, 0)
    send_own(ORDER[2:])
    q_copy.wait()

    def attend(g, dist):
        lanes = slice(g * 128, (g + 1) * 128)

        def one(r, _):
            h = g * 8 + r
            q = q_ref[:, pl.ds(pl.multiple_of(h * 128, 128), 128)]
            lhs = jnp.concatenate([q, qaug[...]], axis=1)
            if dist == 0:
                keys, values = k_ref[:, lanes], v_ref[:, lanes]
            else:
                keys, values = kbuf[dist - 1, :, lanes], vbuf[dist - 1, :, lanes]
            s = dot_nt(lhs, jnp.concatenate([keys, kaug[dist]], axis=1))
            if dist == 0:
                qi = lax.broadcasted_iota(jnp.int32, (ROWS, ROWS), 0)
                ki = lax.broadcasted_iota(jnp.int32, (ROWS, ROWS), 1)
                s = jnp.where(qi >= ki, s, -float(FAR))
            top = jnp.max(s, axis=1, keepdims=True)
            if dist == 0:
                new = jnp.broadcast_to(top, (ROWS, 128))
            else:
                old = peak[h]
                new = jnp.maximum(old, top)
            peak[h] = new
            prob = jnp.exp((s - jnp.concatenate([new, new], axis=1)) * SCALE).astype(BF16)
            out = dot(prob, jnp.concatenate([values, jnp.ones((ROWS, 128), BF16)], axis=1))
            if dist:
                back = jnp.exp((old - new) * SCALE)
                out = out + acc[h] * jnp.concatenate([back, back], axis=1)
            acc[h] = out
            return 0

        lax.fori_loop(0, 8, one, 0)

    def finish_ssm(quarter, squares):
        lo_l = quarter * 512
        lanes = slice(lo_l, lo_l + 512)
        state = tbuf[3, :, lanes].astype(F32)
        for dist in (3, 2, 1):
            cw = enter1[dist - 1 : dist, lanes]
            state = tbuf[dist - 1, :, lanes].astype(F32) + cw * state
        g = quarter // 2
        cols = slice(g * 128, (g + 1) * 128)
        later = enter0[0:1, lanes] * state + bs0[:, lanes]
        for i, st in enumerate((state, later)):
            rows = slice(i * BLK, (i + 1) * BLK)
            hi, mid, lo = split3(st)
            cc = c_ref[rows, cols]
            read = dot(jnp.concatenate([cc, cc], axis=1), jnp.concatenate([hi, mid], axis=0)) + dot(cc, lo)
            zz = z_ref[rows, lanes].astype(F32)
            y = intra[rows, lanes] + rgain[rows, lanes] * read
            y = y + enter0[2:3, lanes] * x_ref[rows, lanes].astype(F32)
            gated = y * (zz / (1.0 + jnp.exp(-zz)))
            intra[rows, lanes] = gated
            squares[i] = squares[i] + jnp.sum(gated * gated, axis=1, keepdims=True)
        return squares

    plan = {
        0: [(0, 0), (0, 4), (0, 1)],
        1: [(1, 0), (1, 4), (1, 1), (0, 3)],
        2: [(2, 0), (1, 3)],
        3: [],
        4: [(3, 0), (0, 2)],
        5: [(2, 4), (2, 1), (1, 2)],
        6: [(3, 4), (3, 1), (2, 3)],
        7: [(3, 3)],
        8: [],
    }
    early2 = {4: [(KV, 0)], 5: [(KV, 1)]}
    for i, item in enumerate(ORDER):
        got4(item)
        got1(item)
        if i:
            got3(ORDER[i - 1])
        for it in early2.get(i, ()):
            got2(it)
        for g, dist in plan[i]:
            attend(g, dist)
    got3(ORDER[-1])
    got2((CR, 0))
    rows8 = lax.broadcasted_iota(jnp.int32, (8, 128), 0)
    carries = jnp.where(rows8 == 0, cbuf[0], jnp.where(rows8 == 1, cbuf[1], cbuf[2]))
    enter1[...] = dot(carries, spread[...], HIGH)
    z_copy.wait()
    squares = [jnp.zeros((BLK, 1), F32)] * 2
    for quarter in (0, 1):
        got2((ST, quarter))
        squares = finish_ssm(quarter, squares)
    for g in (2, 3):
        got2((KV, g))
        attend(g, 2)
    for quarter in (2, 3):
        got2((ST, quarter))
        squares = finish_ssm(quarter, squares)
    for i in range(2):
        sq_own[i * BLK : (i + 1) * BLK] = jnp.broadcast_to(squares[i], (BLK, 128))

    sq_copy = pltpu.make_async_remote_copy(
        sq_own, sq_other, qsem.at[0], qsem.at[1], device_id=other, device_id_type=MESH
    )
    sq_copy.start()

    def divide(h, _):
        lanes = pl.ds(pl.multiple_of(h * 128, 128), 128)
        attn_out[:, lanes] = (acc[h, :, 0:128] / acc[h, :, 128:256]).astype(BF16)
        return 0

    lax.fori_loop(0, 32, divide, 0)
    sq_copy.wait()
    for i in range(2):
        rows = slice(i * BLK, (i + 1) * BLK)
        total = (sq_own[rows] + sq_other[rows])[:, 0:1]
        norm = lax.rsqrt(total / CHANNELS + EPS)
        ssm_out[rows] = (intra[rows] * norm * gain_ref[...]).astype(BF16)
    for dist in (1, 2, 3, 4):
        for item in ORDER:
            for copy in send(item, 0, dist, at(4)):
                copy.wait_send()


def per_device(
    ssm_input, gate_input, b_input, c_input, step_size, decay_log, skip_gain, norm_gain, queries, key_rows,
    value_rows, doc_lengths,
):
    vm = pl.BlockSpec(memory_space=pltpu.VMEM)
    hbm = pl.BlockSpec(memory_space=pl.ANY)
    sm = pl.BlockSpec(memory_space=pltpu.SMEM)
    dma = pltpu.SemaphoreType.DMA
    skip = jnp.pad(skip_gain, (0, 96)).reshape(1, 128)
    return pl.pallas_call(
        body,
        out_shape=(
            jax.ShapeDtypeStruct((ROWS, LANES), BF16),
            jax.ShapeDtypeStruct((ROWS, 4096), BF16),
        ),
        in_specs=[sm] + [vm] * 9 + [hbm] * 2,
        out_specs=(vm, vm),
        scratch_shapes=[
            pltpu.VMEM((ROWS, LANES), BF16),
            pltpu.VMEM((ROWS, 4096), BF16),
            pltpu.VMEM((4, ROWS, 512), BF16),
            pltpu.VMEM((4, ROWS, 512), BF16),
            pltpu.VMEM((4, BLK, LANES), BF16),
            pltpu.VMEM((4, 8, 128), F32),
            pltpu.VMEM((BLK, LANES), BF16),
            pltpu.VMEM((8, 128), F32),
            pltpu.VMEM((ROWS, 128), BF16),
            pltpu.VMEM((5, ROWS, 128), BF16),
            pltpu.VMEM((32, ROWS, 256), F32),
            pltpu.VMEM((32, ROWS, 128), F32),
            pltpu.VMEM((ROWS, 128), F32),
            pltpu.VMEM((ROWS, 128), F32),
            pltpu.VMEM((ROWS, 128), F32),
            pltpu.VMEM((ROWS, 128), BF16),
            pltpu.VMEM((2, 128, 128), F32),
            pltpu.VMEM((2, 128, 128), F32),
            pltpu.VMEM((2, 128, 128), F32),
            pltpu.VMEM((4, 128, 128), F32),
            pltpu.VMEM((4, 128, 128), F32),
            pltpu.VMEM((ROWS, LANES), F32),
            pltpu.VMEM((ROWS, LANES), F32),
            pltpu.VMEM((BLK, LANES), F32),
            pltpu.VMEM((BLK, LANES), F32),
            pltpu.VMEM((8, LANES), F32),
            pltpu.VMEM((8, LANES), F32),
            pltpu.VMEM((ROWS, 128), F32),
            pltpu.VMEM((ROWS, 128), F32),
            dma((2,)),
            dma((4, 4, 2)),
            dma((4, 4, 2)),
            dma((4, 5)),
            dma((4, 5)),
            dma((2,)),
        ],
        compiler_params=pltpu.CompilerParams(collective_id=0, has_side_effects=True),
        name="layer",
    )(
        doc_lengths, ssm_input, b_input, c_input, step_size, decay_log, skip, norm_gain.reshape(1, LANES),
        key_rows, value_rows, gate_input, queries,
    )


def solution(mesh):
    both = P("ctx", "head")
    placed = (both,) * 6 + (P("head"),) * 2 + (both,) * 3 + (P(),)
    return jax.shard_map(
        per_device, mesh=mesh, in_specs=placed, out_specs=(both, both), check_vma=False
    )
```

```python
import math

import jax
import jax.numpy as jnp
from jax import lax
from jax.experimental import pallas as pl
from jax.experimental.pallas import tpu as pltpu
from jax.sharding import PartitionSpec as P

ROWS = 256
BLK = 128
HP = 64
PAIRS = 16
LANES = 2048
EPS = 1e-05
CHANNELS = 4096
FAR = 2**30
SCALE2 = math.log2(math.e) / math.sqrt(128.0)
UNROLL = 4
F32 = jnp.float32
BF16 = jnp.bfloat16
HIGH = lax.Precision.HIGHEST
MESH = pl.DeviceIdType.MESH
NT = (((1,), (1,)), ((), ()))
KV, ST, CR = 0, 1, 2
ORDER = ((KV, 0), (KV, 1), (KV, 2), (CR, 0), (ST, 0), (ST, 1), (KV, 3), (ST, 2), (ST, 3))
LEFT = ((KV, 0), (KV, 1), (ST, 0), (ST, 1))


def dot(a, b, precision=None):
    return jnp.dot(a, b, preferred_element_type=F32, precision=precision)


def dot_nt(a, b):
    return lax.dot_general(a, b, NT, preferred_element_type=F32)


def split3(v):
    hi = v.astype(BF16)
    rest = v - hi.astype(F32)
    mid = rest.astype(BF16)
    return hi, mid, (rest - mid.astype(F32)).astype(BF16)


def body(
    doc_ref, x_ref, b_ref, c_ref, step_ref, decay_ref, skip_ref, gain_ref, k_ref, v_ref, z_hbm, q_hbm,
    ssm_out, attn_out,
    z_ref, q_ref, kbuf, vbuf, tbuf, cbuf, town, cown, qaug, kaug, acc, peak,
    dpad, spad, skip_pad, cum3, cum_t, step_t, end_t, scm, bt, intra, rgain, spread, bs0, enter0, enter1,
    sq_own, sq_other,
    lsem, kvs, kvr, sts, str_, qsem,
):
    d = lax.axis_index("ctx")
    head = lax.axis_index("head")
    n = lax.axis_size("ctx")
    x = lax.rem(d, 4)

    def at(off):
        return {"ctx": lax.rem(d + off + n, n)}

    right = {"ctx": jnp.where(x == 3, d - 3, d + 1)}
    left = {"ctx": jnp.where(x == 0, d + 3, d - 1)}
    other = {"head": 1 - head}
    z_copy = pltpu.make_async_copy(z_hbm, z_ref, lsem.at[0])
    q_copy = pltpu.make_async_copy(q_hbm, q_ref, lsem.at[1])
    q_copy.start()
    z_copy.start()
    barrier = pltpu.get_barrier_semaphore()
    for peer in (at(4), at(-4), at(1), at(-1), right, left, other):
        pl.semaphore_signal(barrier, inc=1, device_id=peer, device_id_type=MESH)
    pl.semaphore_wait(barrier, 7)

    def send(item, src, dist, to):
        kind, i = item
        s, r = dist - 1, dist - 1
        if kind == KV:
            lanes = pl.ds(i * 128, 128)
            pairs = ((k_ref, kbuf, 0), (v_ref, vbuf, 1))
            return [
                pltpu.make_async_remote_copy(
                    own.at[:, lanes] if src == 0 else buf.at[src - 1, :, lanes],
                    buf.at[dist - 1, :, lanes],
                    kvs.at[s, i, j], kvr.at[r, i, j], device_id=to, device_id_type=MESH,
                )
                for own, buf, j in pairs
            ]
        if kind == ST:
            lanes = pl.ds(i * 512, 512)
            return [
                pltpu.make_async_remote_copy(
                    town.at[:, lanes] if src == 0 else tbuf.at[src - 1, :, lanes],
                    tbuf.at[dist - 1, :, lanes],
                    sts.at[s, i], str_.at[r, i], device_id=to, device_id_type=MESH,
                )
            ]
        return [
            pltpu.make_async_remote_copy(
                cown if src == 0 else cbuf.at[src - 1], cbuf.at[dist - 1],
                sts.at[s, 4], str_.at[r, 4], device_id=to, device_id_type=MESH,
            )
        ]

    def start(copies):
        for copy in copies:
            copy.start()

    def arrive(item, dist):
        for copy in send(item, 0, dist, at(4)):
            copy.wait_recv()

    def send_own(items):
        for item in items:
            start(send(item, 0, 4, at(4)))

        @pl.when(x < 3)
        def _():
            for item in items:
                start(send(item, 0, 1, right))

        @pl.when(x == 0)
        def _():
            for item in items:
                start(send(item, 0, 3, left))

    def got4(item):
        arrive(item, 4)

        @pl.when(x > 0)
        def _():
            start(send(item, 4, 3, left))

        @pl.when(x == 3)
        def _():
            start(send(item, 4, 1, right))

    def got1(item):
        arrive(item, 1)
        if item not in LEFT:
            start(send(item, 1, 2, at(1)))

    def got3(item):
        arrive(item, 3)
        if item in LEFT:
            start(send(item, 3, 2, at(-1)))

    def got2(item):
        arrive(item, 2)

    send_own(ORDER[:3])

    lane = lax.broadcasted_iota(jnp.int32, (1, 128), 1)

    def one_doc(j, carry):
        run, first, last = carry
        length = doc_ref[j]
        first = jnp.where(lane == j, run, first)
        last = jnp.where(lane == j, run + length, last)
        return run + length, first, last

    first0 = jnp.where(lane == 127, -FAR, FAR)
    last0 = jnp.where(lane == 127, 0, -FAR)
    _, first, last = lax.fori_loop(0, 32, one_doc, (jnp.int32(0), first0, last0))

    def marks(base, rows):
        pos = base + lax.broadcasted_iota(jnp.int32, (rows, 128), 0)
        return jnp.where((pos >= first) & (pos < last), 1.0, 0.0).astype(F32)

    row0 = d * ROWS
    own_marks = marks(row0, ROWS)
    qaug[...] = ((own_marks - 1.0) * float(FAR)).astype(BF16)
    for j in range(5):
        kaug[j] = (own_marks if j == 0 else marks(row0 - j * ROWS, ROWS)).astype(BF16)

    dpad[...] = jnp.zeros_like(dpad)
    spad[...] = jnp.zeros_like(spad)
    dpad[0:32] = decay_ref[...]
    spad[0:32] = step_ref[...]
    ti = lax.broadcasted_iota(jnp.int32, (BLK, BLK), 0)
    si = lax.broadcasted_iota(jnp.int32, (BLK, BLK), 1)
    causal = ti >= si
    tri = causal.astype(F32)
    shift = [
        ((si == ti + 32 * k) & (ti < 32)).astype(BF16) for k in range(3)
    ]
    spread_i = lax.broadcasted_iota(jnp.int32, (BLK, LANES), 0)
    spread_l = lax.broadcasted_iota(jnp.int32, (BLK, LANES), 1)
    spread[...] = jnp.where(lax.shift_right_logical(spread_l, 6) == spread_i, 1.0, 0.0).astype(BF16)

    def widen(rows8):
        hi, mid, lo = split3(jnp.concatenate([rows8, jnp.zeros_like(rows8)], axis=0))
        wide3 = dot(jnp.concatenate([hi, mid, lo], axis=0), spread[...])
        return wide3[0:8] + wide3[16:24] + wide3[32:40]

    carry_total = jnp.where(lane < 32, 1.0, 0.0)
    carry_rows = []
    for i in range(2):
        rows = slice(i * BLK, (i + 1) * BLK)
        oh = own_marks[rows]
        before = marks(row0 + i * BLK - 1, 8)[0:1]
        oh_last = oh[BLK - 1 : BLK]
        ct = lax.dot_general(dpad[:, rows], tri, NT, preferred_element_type=F32, precision=HIGH)
        cum = ct.T
        cum_t[i] = ct
        stt = spad[:, rows]
        step_t[i] = stt
        ohb = oh.astype(BF16)
        same = dot_nt(ohb, ohb)
        allowed = causal & (same > 0.5)
        last_row = same[BLK - 1 : BLK]
        end_t[i] = jnp.exp(ct[:, BLK - 1 : BLK] - ct) * last_row * stt
        for g in range(2):
            cols = slice(g * 128, (g + 1) * 128)
            sc = dot_nt(c_ref[rows, cols], b_ref[rows, cols])
            scm[2 * i + g] = jnp.where(allowed, sc, 0.0)
            bt[2 * i + g] = b_ref[rows, cols].astype(F32).T
        hi, mid, lo = split3(cum)
        cum3[rows] = (dot(hi, shift[0]) + dot(mid, shift[1]) + dot(lo, shift[2])).astype(BF16)
        joined = jnp.sum(oh_last * before, axis=1, keepdims=True)
        gain_row = jnp.where(lane < 32, jnp.exp(cum[BLK - 1 : BLK]) * joined, 0.0)
        carry_rows.append(gain_row)
        carry_total = carry_total * gain_row
        reads = jnp.sum(oh * before, axis=1, keepdims=True)
        rg = jnp.exp(cum) * reads
        rhi = rg.astype(BF16)
        rlo = (rg - rhi.astype(F32)).astype(BF16)
        rgain[rows] = dot(rhi, spread[...]) + dot(rlo, spread[...])
    cown[...] = jnp.broadcast_to(carry_total, (8, 128))
    row_id = lax.broadcasted_iota(jnp.int32, (8, 128), 0)
    skip_pad[...] = jnp.zeros_like(skip_pad)
    skip_pad[:, 0:32] = jnp.broadcast_to(skip_ref[...], (8, 32))
    small = jnp.where(row_id == 0, carry_rows[0], jnp.where(row_id == 1, carry_rows[1], skip_pad[...]))
    wide = widen(small)
    start_lane = lax.broadcasted_iota(jnp.int32, (BLK, 256), 1)
    start_row = lax.broadcasted_iota(jnp.int32, (BLK, 256), 0)
    low = lax.broadcasted_iota(jnp.int32, (BLK, BLK), 1) < HP
    enter0[0:8] = wide

    def pair(p, _):
        lanes = pl.ds(pl.multiple_of(p * 128, 128), 128)
        pick = jnp.where(
            ((start_row & 31) == 2 * p + lax.shift_right_logical(start_lane, 7)) & (start_row < 96), 1.0, 0.0
        ).astype(BF16)
        cols = dot(cum3[...], pick)
        g = lax.shift_right_logical(p, 3)
        outs = []
        for i in range(2):
            xs = x_ref[i * BLK : (i + 1) * BLK, lanes]
            parts = []
            sg = scm[2 * i + g]
            bg = bt[2 * i + g]
            for e in range(2):
                crow = cum_t[i, pl.ds(2 * p + e, 1), :]
                srow = step_t[i, pl.ds(2 * p + e, 1), :]
                diff = jnp.minimum(cols[i * BLK : (i + 1) * BLK, e * 128 : (e + 1) * 128] - crow, 0.0)
                parts.append((sg * jnp.exp(diff) * srow).astype(BF16))
            for e in range(2):
                erow = end_t[i, pl.ds(2 * p + e, 1), :]
                parts.append((bg * erow).astype(BF16))
            res = dot(jnp.concatenate(parts, axis=0), xs)
            intra[i * BLK : (i + 1) * BLK, lanes] = jnp.where(low, res[0:128], res[128:256])
            outs.append(jnp.where(low, res[256:384], res[384:512]))
        bs0[:, lanes] = outs[0]
        c1 = enter0[1:2, lanes]
        town[:, lanes] = (c1 * outs[0] + outs[1]).astype(BF16)
        return 0

    lax.fori_loop(0, PAIRS, pair, 0)
    send_own(ORDER[3:6])
    q_copy.wait()

    def attend(g, parts, first_time):
        lanes = slice(g * 128, (g + 1) * 128)
        for half in range(2):
            rows = slice(half * BLK, (half + 1) * BLK)

            def one(r, _):
                h = g * 8 + 2 * r
                slot = half * 16 + g * 4 + r
                qs, ks, vs, ms = [], [], [], []
                for e in range(2):
                    q = q_ref[rows, pl.ds(pl.multiple_of((h + e) * 128, 128), 128)]
                    qs.append(jnp.concatenate([q, qaug[rows]], axis=1))
                for dist, a, b in parts[half]:
                    if dist == 0:
                        keys, values = k_ref[a:b, lanes], v_ref[a:b, lanes]
                    else:
                        keys, values = kbuf[dist - 1, a:b, lanes], vbuf[dist - 1, a:b, lanes]
                    ks.append(jnp.concatenate([keys, kaug[dist, a:b]], axis=1))
                    vs.append(values)
                values = jnp.concatenate(vs, axis=0)
                s = dot_nt(jnp.concatenate(qs, axis=0), jnp.concatenate(ks, axis=0))
                if first_time:
                    at0 = half * BLK
                    qi = lax.broadcasted_iota(jnp.int32, (2 * BLK, BLK), 0) & (BLK - 1)
                    ki = lax.broadcasted_iota(jnp.int32, (2 * BLK, BLK), 1)
                    diag = jnp.where(qi >= ki, s[:, at0 : at0 + BLK], -float(FAR))
                    pieces = ([s[:, :at0]] if at0 else []) + [diag, s[:, at0 + BLK :]]
                    s = jnp.concatenate(pieces, axis=1)
                top = jnp.max(s, axis=1, keepdims=True)
                if first_time:
                    new = jnp.broadcast_to(top, (2 * BLK, 128))
                else:
                    old = peak[slot]
                    new = jnp.maximum(old, top)
                peak[slot] = new
                wide_new = jnp.concatenate([new] * (s.shape[1] // 128), axis=1)
                prob = jnp.exp2((s - wide_new) * SCALE2).astype(BF16)
                ones = jnp.ones((values.shape[0], 128), BF16)
                out = dot(prob, jnp.concatenate([values, ones], axis=1))
                if not first_time:
                    back = jnp.exp2((old - new) * SCALE2)
                    out = out + acc[slot] * jnp.concatenate([back, back], axis=1)
                acc[slot] = out
                return 0

            lax.fori_loop(0, 4, one, 0, unroll=UNROLL)

    near = (
        ((0, 0, 128), (4, 0, 256), (1, 0, 256)),
        ((0, 0, 256), (4, 128, 256), (1, 0, 256)),
    )
    rest = (((3, 0, 256), (2, 0, 256)),) * 2

    def finish_ssm(quarter, squares):
        lo_l = quarter * 512
        lanes = slice(lo_l, lo_l + 512)
        state = tbuf[3, :, lanes].astype(F32)
        for dist in (3, 2, 1):
            cw = enter1[dist - 1 : dist, lanes]
            state = tbuf[dist - 1, :, lanes].astype(F32) + cw * state
        g = quarter // 2
        cols = slice(g * 128, (g + 1) * 128)
        later = enter0[0:1, lanes] * state + bs0[:, lanes]
        for i, st in enumerate((state, later)):
            rows = slice(i * BLK, (i + 1) * BLK)
            hi = st.astype(BF16)
            mid = (st - hi.astype(F32)).astype(BF16)
            cc = c_ref[rows, cols]
            read = dot(jnp.concatenate([cc, cc], axis=1), jnp.concatenate([hi, mid], axis=0))
            zz = z_ref[rows, lanes].astype(F32)
            y = intra[rows, lanes] + rgain[rows, lanes] * read
            y = y + enter0[2:3, lanes] * x_ref[rows, lanes].astype(F32)
            gated = y * (zz / (1.0 + jnp.exp(-zz)))
            intra[rows, lanes] = gated
            squares[i] = squares[i] + jnp.sum(gated * gated, axis=1, keepdims=True)
        return squares

    near_at = {0: 0, 1: 1, 2: 2, 6: 3}
    rest_at = {7: 0, 8: 1}
    for i, item in enumerate(ORDER):
        got4(item)
        got1(item)
        if i:
            got3(ORDER[i - 1])
        if i < 3:
            send_own(ORDER[6 + i : 7 + i])
        if i in near_at:
            attend(near_at[i], near, True)
        if i in rest_at:
            got2((KV, rest_at[i]))
            attend(rest_at[i], rest, False)
    got3(ORDER[-1])
    got2((CR, 0))
    rows8 = lax.broadcasted_iota(jnp.int32, (8, 128), 0)
    carries = jnp.where(rows8 == 0, cbuf[0], jnp.where(rows8 == 1, cbuf[1], cbuf[2]))
    enter1[...] = widen(carries)
    z_copy.wait()
    squares = [jnp.zeros((BLK, 1), F32)] * 2
    for quarter in (0, 1):
        got2((ST, quarter))
        squares = finish_ssm(quarter, squares)
    for g in (2, 3):
        got2((KV, g))
        attend(g, rest, False)
    for quarter in (2, 3):
        got2((ST, quarter))
        squares = finish_ssm(quarter, squares)
    for i in range(2):
        sq_own[i * BLK : (i + 1) * BLK] = jnp.broadcast_to(squares[i], (BLK, 128))

    sq_copy = pltpu.make_async_remote_copy(
        sq_own, sq_other, qsem.at[0], qsem.at[1], device_id=other, device_id_type=MESH
    )
    sq_copy.start()

    def divide(t, _):
        for half in range(2):
            rows = slice(half * BLK, (half + 1) * BLK)
            slot = half * 16 + t
            for e in range(2):
                part = slice(e * BLK, (e + 1) * BLK)
                lanes = pl.ds(pl.multiple_of((2 * t + e) * 128, 128), 128)
                attn_out[rows, lanes] = (acc[slot, part, 0:128] / acc[slot, part, 128:256]).astype(BF16)
        return 0

    lax.fori_loop(0, 16, divide, 0)
    sq_copy.wait()
    for i in range(2):
        rows = slice(i * BLK, (i + 1) * BLK)
        total = (sq_own[rows] + sq_other[rows])[:, 0:1]
        norm = lax.rsqrt(total / CHANNELS + EPS)
        ssm_out[rows] = (intra[rows] * norm * gain_ref[...]).astype(BF16)
    for dist in (1, 2, 3, 4):
        for item in ORDER:
            for copy in send(item, 0, dist, at(4)):
                copy.wait_send()


def per_device(
    ssm_input, gate_input, b_input, c_input, step_size, decay_log, skip_gain, norm_gain, queries, key_rows,
    value_rows, doc_lengths,
):
    vm = pl.BlockSpec(memory_space=pltpu.VMEM)
    hbm = pl.BlockSpec(memory_space=pl.ANY)
    sm = pl.BlockSpec(memory_space=pltpu.SMEM)
    dma = pltpu.SemaphoreType.DMA
    skip = skip_gain.reshape(1, 32)
    return pl.pallas_call(
        body,
        out_shape=(
            jax.ShapeDtypeStruct((ROWS, LANES), BF16),
            jax.ShapeDtypeStruct((ROWS, 4096), BF16),
        ),
        in_specs=[sm] + [vm] * 9 + [hbm] * 2,
        out_specs=(vm, vm),
        scratch_shapes=[
            pltpu.VMEM((ROWS, LANES), BF16),
            pltpu.VMEM((ROWS, 4096), BF16),
            pltpu.VMEM((4, ROWS, 512), BF16),
            pltpu.VMEM((4, ROWS, 512), BF16),
            pltpu.VMEM((4, BLK, LANES), BF16),
            pltpu.VMEM((4, 8, 128), F32),
            pltpu.VMEM((BLK, LANES), BF16),
            pltpu.VMEM((8, 128), F32),
            pltpu.VMEM((ROWS, 128), BF16),
            pltpu.VMEM((5, ROWS, 128), BF16),
            pltpu.VMEM((32, ROWS, 256), F32),
            pltpu.VMEM((32, ROWS, 128), F32),
            pltpu.VMEM((128, ROWS), F32),
            pltpu.VMEM((128, ROWS), F32),
            pltpu.VMEM((8, 128), F32),
            pltpu.VMEM((ROWS, 128), BF16),
            pltpu.VMEM((2, 128, 128), F32),
            pltpu.VMEM((2, 128, 128), F32),
            pltpu.VMEM((2, 128, 128), F32),
            pltpu.VMEM((4, 128, 128), F32),
            pltpu.VMEM((4, 128, 128), F32),
            pltpu.VMEM((ROWS, LANES), F32),
            pltpu.VMEM((ROWS, LANES), F32),
            pltpu.VMEM((BLK, LANES), BF16),
            pltpu.VMEM((BLK, LANES), F32),
            pltpu.VMEM((8, LANES), F32),
            pltpu.VMEM((8, LANES), F32),
            pltpu.VMEM((ROWS, 128), F32),
            pltpu.VMEM((ROWS, 128), F32),
            dma((2,)),
            dma((4, 4, 2)),
            dma((4, 4, 2)),
            dma((4, 5)),
            dma((4, 5)),
            dma((2,)),
        ],
        compiler_params=pltpu.CompilerParams(collective_id=0, has_side_effects=True),
        name="layer",
    )(
        doc_lengths, ssm_input, b_input, c_input, step_size.T, decay_log.T, skip, norm_gain.reshape(1, LANES),
        key_rows, value_rows, gate_input, queries,
    )


def solution(mesh):
    both = P("ctx", "head")
    placed = (both,) * 6 + (P("head"),) * 2 + (both,) * 3 + (P(),)
    return jax.shard_map(
        per_device, mesh=mesh, in_specs=placed, out_specs=(both, both), check_vma=False
    )
```

```python
import math

import jax
import jax.numpy as jnp
from jax import lax
from jax.experimental import pallas as pl
from jax.experimental.pallas import tpu as pltpu
from jax.sharding import PartitionSpec as P

ROWS = 256
BLK = 128
HP = 64
PAIRS = 16
LANES = 2048
EPS = 1e-05
CHANNELS = 4096
FAR = 2**30
SCALE2 = math.log2(math.e) / math.sqrt(128.0)
UNROLL = 4
F32 = jnp.float32
BF16 = jnp.bfloat16
HIGH = lax.Precision.HIGHEST
MESH = pl.DeviceIdType.MESH
NT = (((1,), (1,)), ((), ()))
KV, ST, CR = 0, 1, 2
ORDER = ((KV, 0), (KV, 1), (KV, 2), (CR, 0), (ST, 0), (ST, 1), (ST, 2), (ST, 3), (KV, 3))
LEFT = ((KV, 0), (KV, 1), (ST, 0), (ST, 1))


def dot(a, b, precision=None):
    return jnp.dot(a, b, preferred_element_type=F32, precision=precision)


def dot_nt(a, b):
    return lax.dot_general(a, b, NT, preferred_element_type=F32)


def split3(v):
    hi = v.astype(BF16)
    rest = v - hi.astype(F32)
    mid = rest.astype(BF16)
    return hi, mid, (rest - mid.astype(F32)).astype(BF16)


def body(
    doc_ref, x_ref, b_ref, c_ref, step_ref, decay_ref, skip_ref, gain_ref, k_ref, v_ref, z_hbm, q_hbm,
    ssm_out, attn_out,
    z_ref, q_ref, kbuf, vbuf, tbuf, cbuf, town, cown, qaug, kaug, acc, peak,
    dpad, spad, skip_pad, cum3, cum_t, step_t, end_t, scm, bt, intra, rgain, spread, bs0, enter0, enter1,
    sq_own, sq_other,
    lsem, kvs, kvr, sts, str_, qsem,
):
    d = lax.axis_index("ctx")
    head = lax.axis_index("head")
    n = lax.axis_size("ctx")
    x = lax.rem(d, 4)

    def at(off):
        return {"ctx": lax.rem(d + off + n, n)}

    right = {"ctx": jnp.where(x == 3, d - 3, d + 1)}
    left = {"ctx": jnp.where(x == 0, d + 3, d - 1)}
    other = {"head": 1 - head}
    z_copy = pltpu.make_async_copy(z_hbm, z_ref, lsem.at[0])
    q_copy = pltpu.make_async_copy(q_hbm, q_ref, lsem.at[1])
    q_copy.start()
    z_copy.start()
    barrier = pltpu.get_barrier_semaphore()
    for peer in (at(4), at(-4), at(1), at(-1), right, left, other):
        pl.semaphore_signal(barrier, inc=1, device_id=peer, device_id_type=MESH)
    pl.semaphore_wait(barrier, 7)

    def send(item, src, dist, to):
        kind, i = item
        s, r = dist - 1, dist - 1
        if kind == KV:
            lanes = pl.ds(i * 128, 128)
            pairs = ((k_ref, kbuf, 0), (v_ref, vbuf, 1))
            return [
                pltpu.make_async_remote_copy(
                    own.at[:, lanes] if src == 0 else buf.at[src - 1, :, lanes],
                    buf.at[dist - 1, :, lanes],
                    kvs.at[s, i, j], kvr.at[r, i, j], device_id=to, device_id_type=MESH,
                )
                for own, buf, j in pairs
            ]
        if kind == ST:
            lanes = pl.ds(i * 512, 512)
            return [
                pltpu.make_async_remote_copy(
                    town.at[:, lanes] if src == 0 else tbuf.at[src - 1, :, lanes],
                    tbuf.at[dist - 1, :, lanes],
                    sts.at[s, i], str_.at[r, i], device_id=to, device_id_type=MESH,
                )
            ]
        return [
            pltpu.make_async_remote_copy(
                cown if src == 0 else cbuf.at[src - 1], cbuf.at[dist - 1],
                sts.at[s, 4], str_.at[r, 4], device_id=to, device_id_type=MESH,
            )
        ]

    def start(copies):
        for copy in copies:
            copy.start()

    def arrive(item, dist):
        for copy in send(item, 0, dist, at(4)):
            copy.wait_recv()

    def send_own(items):
        for item in items:
            start(send(item, 0, 4, at(4)))

        @pl.when(x < 3)
        def _():
            for item in items:
                start(send(item, 0, 1, right))

        @pl.when(x == 0)
        def _():
            for item in items:
                start(send(item, 0, 3, left))

    def got4(item):
        arrive(item, 4)

        @pl.when(x > 0)
        def _():
            start(send(item, 4, 3, left))

        @pl.when(x == 3)
        def _():
            start(send(item, 4, 1, right))

    def got1(item):
        arrive(item, 1)
        if item not in LEFT:
            start(send(item, 1, 2, at(1)))

    def got3(item):
        arrive(item, 3)
        if item in LEFT:
            start(send(item, 3, 2, at(-1)))

    def got2(item):
        arrive(item, 2)

    send_own(ORDER[:3])

    lane = lax.broadcasted_iota(jnp.int32, (1, 128), 1)

    def one_doc(j, carry):
        run, first, last = carry
        length = doc_ref[j]
        first = jnp.where(lane == j, run, first)
        last = jnp.where(lane == j, run + length, last)
        return run + length, first, last

    first0 = jnp.where(lane == 127, -FAR, FAR)
    last0 = jnp.where(lane == 127, 0, -FAR)
    _, first, last = lax.fori_loop(0, 32, one_doc, (jnp.int32(0), first0, last0))

    def marks(base, rows):
        pos = base + lax.broadcasted_iota(jnp.int32, (rows, 128), 0)
        return jnp.where((pos >= first) & (pos < last), 1.0, 0.0).astype(F32)

    row0 = d * ROWS
    own_marks = marks(row0, ROWS)
    qaug[...] = ((own_marks - 1.0) * float(FAR)).astype(BF16)
    for j in range(5):
        kaug[j] = (own_marks if j == 0 else marks(row0 - j * ROWS, ROWS)).astype(BF16)

    dpad[...] = jnp.zeros_like(dpad)
    spad[...] = jnp.zeros_like(spad)
    dpad[0:32] = decay_ref[...]
    spad[0:32] = step_ref[...]
    ti = lax.broadcasted_iota(jnp.int32, (BLK, BLK), 0)
    si = lax.broadcasted_iota(jnp.int32, (BLK, BLK), 1)
    causal = ti >= si
    tri = causal.astype(F32)
    shift = [
        ((si == ti + 32 * k) & (ti < 32)).astype(BF16) for k in range(3)
    ]
    spread_i = lax.broadcasted_iota(jnp.int32, (BLK, LANES), 0)
    spread_l = lax.broadcasted_iota(jnp.int32, (BLK, LANES), 1)
    spread[...] = jnp.where(lax.shift_right_logical(spread_l, 6) == spread_i, 1.0, 0.0).astype(BF16)

    def widen(rows8):
        hi, mid, lo = split3(jnp.concatenate([rows8, jnp.zeros_like(rows8)], axis=0))
        wide3 = dot(jnp.concatenate([hi, mid, lo], axis=0), spread[...])
        return wide3[0:8] + wide3[16:24] + wide3[32:40]

    carry_total = jnp.where(lane < 32, 1.0, 0.0)
    carry_rows = []
    for i in range(2):
        rows = slice(i * BLK, (i + 1) * BLK)
        oh = own_marks[rows]
        before = marks(row0 + i * BLK - 1, 8)[0:1]
        oh_last = oh[BLK - 1 : BLK]
        ct = lax.dot_general(dpad[:, rows], tri, NT, preferred_element_type=F32, precision=HIGH)
        cum = ct.T
        cum_t[i] = ct
        stt = spad[:, rows]
        step_t[i] = stt
        ohb = oh.astype(BF16)
        same = dot_nt(ohb, ohb)
        allowed = causal & (same > 0.5)
        last_row = same[BLK - 1 : BLK]
        end_t[i] = jnp.exp(ct[:, BLK - 1 : BLK] - ct) * last_row * stt
        for g in range(2):
            cols = slice(g * 128, (g + 1) * 128)
            sc = dot_nt(c_ref[rows, cols], b_ref[rows, cols])
            scm[2 * i + g] = jnp.where(allowed, sc, 0.0)
            bt[2 * i + g] = b_ref[rows, cols].astype(F32).T
        hi, mid, lo = split3(cum)
        cum3[rows] = (dot(hi, shift[0]) + dot(mid, shift[1]) + dot(lo, shift[2])).astype(BF16)
        joined = jnp.sum(oh_last * before, axis=1, keepdims=True)
        gain_row = jnp.where(lane < 32, jnp.exp(cum[BLK - 1 : BLK]) * joined, 0.0)
        carry_rows.append(gain_row)
        carry_total = carry_total * gain_row
        reads = jnp.sum(oh * before, axis=1, keepdims=True)
        rg = jnp.exp(cum) * reads
        rhi = rg.astype(BF16)
        rlo = (rg - rhi.astype(F32)).astype(BF16)
        rgain[rows] = dot(rhi, spread[...]) + dot(rlo, spread[...])
    cown[...] = jnp.broadcast_to(carry_total, (8, 128))
    row_id = lax.broadcasted_iota(jnp.int32, (8, 128), 0)
    skip_pad[...] = jnp.zeros_like(skip_pad)
    skip_pad[:, 0:32] = jnp.broadcast_to(skip_ref[...], (8, 32))
    small = jnp.where(row_id == 0, carry_rows[0], jnp.where(row_id == 1, carry_rows[1], skip_pad[...]))
    wide = widen(small)
    start_lane = lax.broadcasted_iota(jnp.int32, (BLK, 256), 1)
    start_row = lax.broadcasted_iota(jnp.int32, (BLK, 256), 0)
    low = lax.broadcasted_iota(jnp.int32, (BLK, BLK), 1) < HP
    enter0[0:8] = wide

    def pair(p, _):
        lanes = pl.ds(pl.multiple_of(p * 128, 128), 128)
        pick = jnp.where(
            ((start_row & 31) == 2 * p + lax.shift_right_logical(start_lane, 7)) & (start_row < 96), 1.0, 0.0
        ).astype(BF16)
        cols = dot(cum3[...], pick)
        g = lax.shift_right_logical(p, 3)
        outs = []
        for i in range(2):
            xs = x_ref[i * BLK : (i + 1) * BLK, lanes]
            parts = []
            sg = scm[2 * i + g]
            bg = bt[2 * i + g]
            for e in range(2):
                crow = cum_t[i, pl.ds(2 * p + e, 1), :]
                srow = step_t[i, pl.ds(2 * p + e, 1), :]
                diff = jnp.minimum(cols[i * BLK : (i + 1) * BLK, e * 128 : (e + 1) * 128] - crow, 0.0)
                parts.append((sg * jnp.exp(diff) * srow).astype(BF16))
            for e in range(2):
                erow = end_t[i, pl.ds(2 * p + e, 1), :]
                parts.append((bg * erow).astype(BF16))
            res = dot(jnp.concatenate(parts, axis=0), xs)
            intra[i * BLK : (i + 1) * BLK, lanes] = jnp.where(low, res[0:128], res[128:256])
            outs.append(jnp.where(low, res[256:384], res[384:512]))
        bs0[:, lanes] = outs[0]
        c1 = enter0[1:2, lanes]
        town[:, lanes] = (c1 * outs[0] + outs[1]).astype(BF16)
        return 0

    lax.fori_loop(0, PAIRS, pair, 0)
    send_own(ORDER[3:6])
    q_copy.wait()

    def attend(g, parts, first_time):
        lanes = slice(g * 128, (g + 1) * 128)
        for half in range(2):
            rows = slice(half * BLK, (half + 1) * BLK)

            def one(r, _):
                h = g * 8 + 2 * r
                slot = half * 16 + g * 4 + r
                qs, ks, vs, ms = [], [], [], []
                for e in range(2):
                    q = q_ref[rows, pl.ds(pl.multiple_of((h + e) * 128, 128), 128)]
                    qs.append(jnp.concatenate([q, qaug[rows]], axis=1))
                for dist, a, b in parts[half]:
                    if dist == 0:
                        keys, values = k_ref[a:b, lanes], v_ref[a:b, lanes]
                    else:
                        keys, values = kbuf[dist - 1, a:b, lanes], vbuf[dist - 1, a:b, lanes]
                    ks.append(jnp.concatenate([keys, kaug[dist, a:b]], axis=1))
                    vs.append(values)
                values = jnp.concatenate(vs, axis=0)
                s = dot_nt(jnp.concatenate(qs, axis=0), jnp.concatenate(ks, axis=0))
                if first_time:
                    at0 = half * BLK
                    qi = lax.broadcasted_iota(jnp.int32, (2 * BLK, BLK), 0) & (BLK - 1)
                    ki = lax.broadcasted_iota(jnp.int32, (2 * BLK, BLK), 1)
                    diag = jnp.where(qi >= ki, s[:, at0 : at0 + BLK], -float(FAR))
                    pieces = ([s[:, :at0]] if at0 else []) + [diag, s[:, at0 + BLK :]]
                    s = jnp.concatenate(pieces, axis=1)
                top = jnp.max(s, axis=1, keepdims=True)
                if first_time:
                    new = jnp.broadcast_to(top, (2 * BLK, 128))
                else:
                    old = peak[slot]
                    new = jnp.maximum(old, top)
                if first_time:
                    peak[slot] = new
                wide_new = jnp.concatenate([new] * (s.shape[1] // 128), axis=1)
                prob = jnp.exp2((s - wide_new) * SCALE2).astype(BF16)
                ones = jnp.ones((values.shape[0], 128), BF16)
                out = dot(prob, jnp.concatenate([values, ones], axis=1))
                if not first_time:
                    back = jnp.exp2((old - new) * SCALE2)
                    out = out + acc[slot] * jnp.concatenate([back, back], axis=1)
                    done = (out[:, 0:128] / out[:, 128:256]).astype(BF16)
                    for e in range(2):
                        lanes_out = pl.ds(pl.multiple_of((h + e) * 128, 128), 128)
                        attn_out[rows, lanes_out] = done[e * BLK : (e + 1) * BLK]
                else:
                    acc[slot] = out
                return 0

            lax.fori_loop(0, 4, one, 0, unroll=UNROLL)

    near = (
        ((0, 0, 128), (4, 0, 256), (1, 0, 256)),
        ((0, 0, 256), (4, 128, 256), (1, 0, 256)),
    )
    rest = (((3, 0, 256), (2, 0, 256)),) * 2

    def finish_ssm(quarter, squares):
        lo_l = quarter * 512
        lanes = slice(lo_l, lo_l + 512)
        state = tbuf[3, :, lanes].astype(F32)
        for dist in (3, 2, 1):
            cw = enter1[dist - 1 : dist, lanes]
            state = tbuf[dist - 1, :, lanes].astype(F32) + cw * state
        g = quarter // 2
        cols = slice(g * 128, (g + 1) * 128)
        later = enter0[0:1, lanes] * state + bs0[:, lanes]
        for i, st in enumerate((state, later)):
            rows = slice(i * BLK, (i + 1) * BLK)
            hi = st.astype(BF16)
            mid = (st - hi.astype(F32)).astype(BF16)
            cc = c_ref[rows, cols]
            read = dot(jnp.concatenate([cc, cc], axis=1), jnp.concatenate([hi, mid], axis=0))
            zz = z_ref[rows, lanes].astype(F32)
            y = intra[rows, lanes] + rgain[rows, lanes] * read
            y = y + enter0[2:3, lanes] * x_ref[rows, lanes].astype(F32)
            gated = y * (zz / (1.0 + jnp.exp(-zz)))
            intra[rows, lanes] = gated
            squares[i] = squares[i] + jnp.sum(gated * gated, axis=1, keepdims=True)
        return squares

    near_at = {0: 0, 1: 1, 2: 2, 8: 3}
    rest_at = {6: 0, 7: 1}
    for i, item in enumerate(ORDER):
        got4(item)
        got1(item)
        if i:
            got3(ORDER[i - 1])
        if i < 3:
            send_own(ORDER[6 + i : 7 + i])
        if i in near_at:
            attend(near_at[i], near, True)
        if i in rest_at:
            got2((KV, rest_at[i]))
            attend(rest_at[i], rest, False)
    got3(ORDER[-1])
    got2((CR, 0))
    rows8 = lax.broadcasted_iota(jnp.int32, (8, 128), 0)
    carries = jnp.where(rows8 == 0, cbuf[0], jnp.where(rows8 == 1, cbuf[1], cbuf[2]))
    enter1[...] = widen(carries)
    z_copy.wait()
    squares = [jnp.zeros((BLK, 1), F32)] * 2
    for quarter in (0, 1):
        got2((ST, quarter))
        squares = finish_ssm(quarter, squares)
    got2((KV, 2))
    attend(2, rest, False)
    for quarter in (2, 3):
        got2((ST, quarter))
        squares = finish_ssm(quarter, squares)
    for i in range(2):
        sq_own[i * BLK : (i + 1) * BLK] = jnp.broadcast_to(squares[i], (BLK, 128))
    sq_copy = pltpu.make_async_remote_copy(
        sq_own, sq_other, qsem.at[0], qsem.at[1], device_id=other, device_id_type=MESH
    )
    got2((KV, 3))
    sq_copy.start()
    attend(3, rest, False)
    sq_copy.wait()
    for i in range(2):
        rows = slice(i * BLK, (i + 1) * BLK)
        total = (sq_own[rows] + sq_other[rows])[:, 0:1]
        norm = lax.rsqrt(total / CHANNELS + EPS)
        ssm_out[rows] = (intra[rows] * norm * gain_ref[...]).astype(BF16)
    for dist in (1, 2, 3, 4):
        for item in ORDER:
            for copy in send(item, 0, dist, at(4)):
                copy.wait_send()


def per_device(
    ssm_input, gate_input, b_input, c_input, step_size, decay_log, skip_gain, norm_gain, queries, key_rows,
    value_rows, doc_lengths,
):
    vm = pl.BlockSpec(memory_space=pltpu.VMEM)
    hbm = pl.BlockSpec(memory_space=pl.ANY)
    sm = pl.BlockSpec(memory_space=pltpu.SMEM)
    dma = pltpu.SemaphoreType.DMA
    skip = skip_gain.reshape(1, 32)
    return pl.pallas_call(
        body,
        out_shape=(
            pltpu.VMEM((ROWS, LANES), BF16),
            pltpu.VMEM((ROWS, 4096), BF16),
        ),
        in_specs=[sm] + [vm] * 9 + [hbm] * 2,
        out_specs=(vm, vm),
        scratch_shapes=[
            pltpu.VMEM((ROWS, LANES), BF16),
            pltpu.VMEM((ROWS, 4096), BF16),
            pltpu.VMEM((4, ROWS, 512), BF16),
            pltpu.VMEM((4, ROWS, 512), BF16),
            pltpu.VMEM((4, BLK, LANES), BF16),
            pltpu.VMEM((4, 8, 128), F32),
            pltpu.VMEM((BLK, LANES), BF16),
            pltpu.VMEM((8, 128), F32),
            pltpu.VMEM((ROWS, 128), BF16),
            pltpu.VMEM((5, ROWS, 128), BF16),
            pltpu.VMEM((32, ROWS, 256), F32),
            pltpu.VMEM((32, ROWS, 128), F32),
            pltpu.VMEM((128, ROWS), F32),
            pltpu.VMEM((128, ROWS), F32),
            pltpu.VMEM((8, 128), F32),
            pltpu.VMEM((ROWS, 128), BF16),
            pltpu.VMEM((2, 128, 128), F32),
            pltpu.VMEM((2, 128, 128), F32),
            pltpu.VMEM((2, 128, 128), F32),
            pltpu.VMEM((4, 128, 128), F32),
            pltpu.VMEM((4, 128, 128), F32),
            pltpu.VMEM((ROWS, LANES), F32),
            pltpu.VMEM((ROWS, LANES), F32),
            pltpu.VMEM((BLK, LANES), BF16),
            pltpu.VMEM((BLK, LANES), F32),
            pltpu.VMEM((8, LANES), F32),
            pltpu.VMEM((8, LANES), F32),
            pltpu.VMEM((ROWS, 128), F32),
            pltpu.VMEM((ROWS, 128), F32),
            dma((2,)),
            dma((4, 4, 2)),
            dma((4, 4, 2)),
            dma((4, 5)),
            dma((4, 5)),
            dma((2,)),
        ],
        compiler_params=pltpu.CompilerParams(collective_id=0, has_side_effects=True),
        name="layer",
    )(
        doc_lengths, ssm_input, b_input, c_input, step_size.T, decay_log.T, skip, norm_gain.reshape(1, LANES),
        key_rows, value_rows, gate_input, queries,
    )


def solution(mesh):
    both = P("ctx", "head")
    placed = (both,) * 6 + (P("head"),) * 2 + (both,) * 3 + (P(),)
    return jax.shard_map(
        per_device, mesh=mesh, in_specs=placed, out_specs=(both, both), check_vma=False
    )
```

```python
import math

import jax
import jax.numpy as jnp
from jax import lax
from jax.experimental import pallas as pl
from jax.experimental.pallas import tpu as pltpu
from jax.sharding import PartitionSpec as P

ROWS = 256
BLK = 128
HP = 64
PAIRS = 16
LANES = 2048
EPS = 1e-05
CHANNELS = 4096
FAR = 2**30
SCALE2 = math.log2(math.e) / math.sqrt(128.0)
UNROLL = 4
F32 = jnp.float32
BF16 = jnp.bfloat16
HIGH = lax.Precision.HIGHEST
MESH = pl.DeviceIdType.MESH
NT = (((1,), (1,)), ((), ()))
KV, ST, CR = 0, 1, 2
ORDER = ((KV, 0), (KV, 1), (KV, 2), (CR, 0), (ST, 0), (ST, 1), (ST, 2), (ST, 3), (KV, 3))
LEFT = ((KV, 0), (KV, 1), (ST, 0), (ST, 1))


def dot(a, b, precision=None):
    return jnp.dot(a, b, preferred_element_type=F32, precision=precision)


def dot_nt(a, b):
    return lax.dot_general(a, b, NT, preferred_element_type=F32)


def split3(v):
    hi = v.astype(BF16)
    rest = v - hi.astype(F32)
    mid = rest.astype(BF16)
    return hi, mid, (rest - mid.astype(F32)).astype(BF16)


def body(
    doc_ref, x_hbm, b_ref, c_ref, step_ref, decay_ref, skip_ref, gain_ref, k_ref, v_ref, z_hbm, q_hbm,
    ssm_out, attn_out,
    x_ref, z_ref, q_ref, kbuf, vbuf, tbuf, cbuf, town, cown, qaug, kaug, acc, peak,
    dpad, spad, skip_pad, cum3, cum_t, step_t, end_t, scm, bt, intra, rgain, spread, bs0, enter0, enter1,
    sq_own, sq_other,
    lsem, kvs, kvr, sts, str_, qsem,
):
    d = lax.axis_index("ctx")
    head = lax.axis_index("head")
    n = lax.axis_size("ctx")
    x = lax.rem(d, 4)

    def at(off):
        return {"ctx": lax.rem(d + off + n, n)}

    right = {"ctx": jnp.where(x == 3, d - 3, d + 1)}
    left = {"ctx": jnp.where(x == 0, d + 3, d - 1)}
    other = {"head": 1 - head}
    z_copy = pltpu.make_async_copy(z_hbm, z_ref, lsem.at[0])
    q_copy = pltpu.make_async_copy(q_hbm, q_ref, lsem.at[1])
    x_copy = pltpu.make_async_copy(x_hbm, x_ref, lsem.at[2])
    x_copy.start()
    q_copy.start()
    z_copy.start()
    barrier = pltpu.get_barrier_semaphore()
    for peer in (at(4), at(-4), at(1), at(-1), right, left, other):
        pl.semaphore_signal(barrier, inc=1, device_id=peer, device_id_type=MESH)
    pl.semaphore_wait(barrier, 7)

    def send(item, src, dist, to):
        kind, i = item
        s, r = dist - 1, dist - 1
        if kind == KV:
            lanes = pl.ds(i * 128, 128)
            pairs = ((k_ref, kbuf, 0), (v_ref, vbuf, 1))
            return [
                pltpu.make_async_remote_copy(
                    own.at[:, lanes] if src == 0 else buf.at[src - 1, :, lanes],
                    buf.at[dist - 1, :, lanes],
                    kvs.at[s, i, j], kvr.at[r, i, j], device_id=to, device_id_type=MESH,
                )
                for own, buf, j in pairs
            ]
        if kind == ST:
            halves = [pl.ds(i * 512 + j * 256, 256) for j in range(2)]
            return [
                pltpu.make_async_remote_copy(
                    town.at[:, lanes] if src == 0 else tbuf.at[src - 1, :, lanes],
                    tbuf.at[dist - 1, :, lanes],
                    sts.at[s, i, j], str_.at[r, i, j], device_id=to, device_id_type=MESH,
                )
                for j, lanes in enumerate(halves)
            ]
        return [
            pltpu.make_async_remote_copy(
                cown if src == 0 else cbuf.at[src - 1], cbuf.at[dist - 1],
                sts.at[s, 4, 0], str_.at[r, 4, 0], device_id=to, device_id_type=MESH,
            )
        ]

    def start(copies):
        for copy in copies:
            copy.start()

    def arrive(item, dist):
        for copy in send(item, 0, dist, at(4)):
            copy.wait_recv()

    def send_own(items):
        for item in items:
            start(send(item, 0, 4, at(4)))

        @pl.when(x < 3)
        def _():
            for item in items:
                start(send(item, 0, 1, right))

        @pl.when(x == 0)
        def _():
            for item in items:
                start(send(item, 0, 3, left))

    def parts_of(item):
        return range(1 if item[0] == CR else 2)

    def got4(item):
        for j in parts_of(item):
            send(item, 0, 4, at(4))[j].wait_recv()

            @pl.when(x > 0)
            def _():
                send(item, 4, 3, left)[j].start()

            @pl.when(x == 3)
            def _():
                send(item, 4, 1, right)[j].start()

    def got1(item):
        for j in parts_of(item):
            send(item, 0, 1, at(4))[j].wait_recv()
            if item not in LEFT:
                send(item, 1, 2, at(1))[j].start()

    def got3(item):
        for j in parts_of(item):
            send(item, 0, 3, at(4))[j].wait_recv()
            if item in LEFT:
                send(item, 3, 2, at(-1))[j].start()

    def got2(item):
        arrive(item, 2)

    send_own(ORDER[:3])

    lane = lax.broadcasted_iota(jnp.int32, (1, 128), 1)

    def one_doc(j, carry):
        run, first, last = carry
        length = doc_ref[j]
        first = jnp.where(lane == j, run, first)
        last = jnp.where(lane == j, run + length, last)
        return run + length, first, last

    first0 = jnp.where(lane == 127, -FAR, FAR)
    last0 = jnp.where(lane == 127, 0, -FAR)
    _, first, last = lax.fori_loop(0, 32, one_doc, (jnp.int32(0), first0, last0))

    def marks(base, rows):
        pos = base + lax.broadcasted_iota(jnp.int32, (rows, 128), 0)
        return jnp.where((pos >= first) & (pos < last), 1.0, 0.0).astype(F32)

    row0 = d * ROWS
    own_marks = marks(row0, ROWS)
    qaug[...] = ((own_marks - 1.0) * float(FAR)).astype(BF16)
    for j in range(5):
        kaug[j] = (own_marks if j == 0 else marks(row0 - j * ROWS, ROWS)).astype(BF16)

    dpad[...] = jnp.zeros_like(dpad)
    spad[...] = jnp.zeros_like(spad)
    dpad[0:32] = decay_ref[...]
    spad[0:32] = step_ref[...]
    ti = lax.broadcasted_iota(jnp.int32, (BLK, BLK), 0)
    si = lax.broadcasted_iota(jnp.int32, (BLK, BLK), 1)
    causal = ti >= si
    tri = causal.astype(F32)
    shift = [
        ((si == ti + 32 * k) & (ti < 32)).astype(BF16) for k in range(3)
    ]
    spread_i = lax.broadcasted_iota(jnp.int32, (BLK, LANES), 0)
    spread_l = lax.broadcasted_iota(jnp.int32, (BLK, LANES), 1)
    spread[...] = jnp.where(lax.shift_right_logical(spread_l, 6) == spread_i, 1.0, 0.0).astype(BF16)

    def widen(rows8):
        hi, mid, lo = split3(jnp.concatenate([rows8, jnp.zeros_like(rows8)], axis=0))
        wide3 = dot(jnp.concatenate([hi, mid, lo], axis=0), spread[...])
        return wide3[0:8] + wide3[16:24] + wide3[32:40]

    carry_total = jnp.where(lane < 32, 1.0, 0.0)
    carry_rows = []
    for i in range(2):
        rows = slice(i * BLK, (i + 1) * BLK)
        oh = own_marks[rows]
        before = marks(row0 + i * BLK - 1, 8)[0:1]
        oh_last = oh[BLK - 1 : BLK]
        ct = lax.dot_general(dpad[:, rows], tri, NT, preferred_element_type=F32, precision=HIGH)
        cum = ct.T
        cum_t[i] = ct
        stt = spad[:, rows]
        step_t[i] = stt
        ohb = oh.astype(BF16)
        same = dot_nt(ohb, ohb)
        allowed = causal & (same > 0.5)
        last_row = same[BLK - 1 : BLK]
        end_t[i] = jnp.exp(ct[:, BLK - 1 : BLK] - ct) * last_row * stt
        for g in range(2):
            cols = slice(g * 128, (g + 1) * 128)
            sc = dot_nt(c_ref[rows, cols], b_ref[rows, cols])
            scm[2 * i + g] = jnp.where(allowed, sc, 0.0)
            bt[2 * i + g] = b_ref[rows, cols].astype(F32).T
        hi, mid, lo = split3(cum)
        cum3[rows] = (dot(hi, shift[0]) + dot(mid, shift[1]) + dot(lo, shift[2])).astype(BF16)
        joined = jnp.sum(oh_last * before, axis=1, keepdims=True)
        gain_row = jnp.where(lane < 32, jnp.exp(cum[BLK - 1 : BLK]) * joined, 0.0)
        carry_rows.append(gain_row)
        carry_total = carry_total * gain_row
        reads = jnp.sum(oh * before, axis=1, keepdims=True)
        rg = jnp.exp(cum) * reads
        rhi = rg.astype(BF16)
        rlo = (rg - rhi.astype(F32)).astype(BF16)
        rgain[rows] = dot(rhi, spread[...]) + dot(rlo, spread[...])
    cown[...] = jnp.broadcast_to(carry_total, (8, 128))
    row_id = lax.broadcasted_iota(jnp.int32, (8, 128), 0)
    skip_pad[...] = jnp.zeros_like(skip_pad)
    skip_pad[:, 0:32] = jnp.broadcast_to(skip_ref[...], (8, 32))
    small = jnp.where(row_id == 0, carry_rows[0], jnp.where(row_id == 1, carry_rows[1], skip_pad[...]))
    wide = widen(small)
    start_lane = lax.broadcasted_iota(jnp.int32, (BLK, 256), 1)
    start_row = lax.broadcasted_iota(jnp.int32, (BLK, 256), 0)
    low = lax.broadcasted_iota(jnp.int32, (BLK, BLK), 1) < HP
    enter0[0:8] = wide

    def pair(p, _):
        lanes = pl.ds(pl.multiple_of(p * 128, 128), 128)
        pick = jnp.where(
            ((start_row & 31) == 2 * p + lax.shift_right_logical(start_lane, 7)) & (start_row < 96), 1.0, 0.0
        ).astype(BF16)
        cols = dot(cum3[...], pick)
        g = lax.shift_right_logical(p, 3)
        outs = []
        for i in range(2):
            xs = x_ref[i * BLK : (i + 1) * BLK, lanes]
            parts = []
            sg = scm[2 * i + g]
            bg = bt[2 * i + g]
            for e in range(2):
                crow = cum_t[i, pl.ds(2 * p + e, 1), :]
                srow = step_t[i, pl.ds(2 * p + e, 1), :]
                diff = jnp.minimum(cols[i * BLK : (i + 1) * BLK, e * 128 : (e + 1) * 128] - crow, 0.0)
                parts.append((sg * jnp.exp(diff) * srow).astype(BF16))
            for e in range(2):
                erow = end_t[i, pl.ds(2 * p + e, 1), :]
                parts.append((bg * erow).astype(BF16))
            res = dot(jnp.concatenate(parts, axis=0), xs)
            intra[i * BLK : (i + 1) * BLK, lanes] = jnp.where(low, res[0:128], res[128:256])
            outs.append(jnp.where(low, res[256:384], res[384:512]))
        bs0[:, lanes] = outs[0]
        c1 = enter0[1:2, lanes]
        town[:, lanes] = (c1 * outs[0] + outs[1]).astype(BF16)
        return 0

    x_copy.wait()
    lax.fori_loop(0, PAIRS, pair, 0, unroll=2)
    send_own(ORDER[3:6])
    q_copy.wait()

    def attend(g, parts, first_time):
        lanes = slice(g * 128, (g + 1) * 128)
        for half in range(2):
            rows = slice(half * BLK, (half + 1) * BLK)

            def one(r, _):
                h = g * 8 + 2 * r
                slot = half * 16 + g * 4 + r
                qs, ks, vs, ms = [], [], [], []
                for e in range(2):
                    q = q_ref[rows, pl.ds(pl.multiple_of((h + e) * 128, 128), 128)]
                    qs.append(jnp.concatenate([q, qaug[rows]], axis=1))
                for dist, a, b in parts[half]:
                    if dist == 0:
                        keys, values = k_ref[a:b, lanes], v_ref[a:b, lanes]
                    else:
                        keys, values = kbuf[dist - 1, a:b, lanes], vbuf[dist - 1, a:b, lanes]
                    ks.append(jnp.concatenate([keys, kaug[dist, a:b]], axis=1))
                    vs.append(values)
                values = jnp.concatenate(vs, axis=0)
                s = dot_nt(jnp.concatenate(qs, axis=0), jnp.concatenate(ks, axis=0))
                if first_time:
                    at0 = half * BLK
                    qi = lax.broadcasted_iota(jnp.int32, (2 * BLK, BLK), 0) & (BLK - 1)
                    ki = lax.broadcasted_iota(jnp.int32, (2 * BLK, BLK), 1)
                    diag = jnp.where(qi >= ki, s[:, at0 : at0 + BLK], -float(FAR))
                    pieces = ([s[:, :at0]] if at0 else []) + [diag, s[:, at0 + BLK :]]
                    s = jnp.concatenate(pieces, axis=1)
                top = jnp.max(s, axis=1, keepdims=True)
                if first_time:
                    new = jnp.broadcast_to(top, (2 * BLK, 128))
                else:
                    old = peak[slot]
                    new = jnp.maximum(old, top)
                if first_time:
                    peak[slot] = new
                wide_new = jnp.concatenate([new] * (s.shape[1] // 128), axis=1)
                prob = jnp.exp2((s - wide_new) * SCALE2).astype(BF16)
                ones = jnp.ones((values.shape[0], 128), BF16)
                out = dot(prob, jnp.concatenate([values, ones], axis=1))
                if not first_time:
                    back = jnp.exp2((old - new) * SCALE2)
                    out = out + acc[slot] * jnp.concatenate([back, back], axis=1)
                    done = (out[:, 0:128] / out[:, 128:256]).astype(BF16)
                    for e in range(2):
                        lanes_out = pl.ds(pl.multiple_of((h + e) * 128, 128), 128)
                        attn_out[rows, lanes_out] = done[e * BLK : (e + 1) * BLK]
                else:
                    acc[slot] = out
                return 0

            lax.fori_loop(0, 4, one, 0, unroll=UNROLL)

    near = (
        ((0, 0, 128), (4, 0, 256), (1, 0, 256)),
        ((0, 0, 256), (4, 128, 256), (1, 0, 256)),
    )
    rest = (((3, 0, 256), (2, 0, 256)),) * 2

    def finish_ssm(quarter, squares):
        lo_l = quarter * 512
        lanes = slice(lo_l, lo_l + 512)
        state = tbuf[3, :, lanes].astype(F32)
        for dist in (3, 2, 1):
            cw = enter1[dist - 1 : dist, lanes]
            state = tbuf[dist - 1, :, lanes].astype(F32) + cw * state
        g = quarter // 2
        cols = slice(g * 128, (g + 1) * 128)
        later = enter0[0:1, lanes] * state + bs0[:, lanes]
        for i, st in enumerate((state, later)):
            rows = slice(i * BLK, (i + 1) * BLK)
            hi = st.astype(BF16)
            mid = (st - hi.astype(F32)).astype(BF16)
            cc = c_ref[rows, cols]
            read = dot(jnp.concatenate([cc, cc], axis=1), jnp.concatenate([hi, mid], axis=0))
            zz = z_ref[rows, lanes].astype(F32)
            y = intra[rows, lanes] + rgain[rows, lanes] * read
            y = y + enter0[2:3, lanes] * x_ref[rows, lanes].astype(F32)
            gated = y * (zz / (1.0 + jnp.exp(-zz)))
            intra[rows, lanes] = gated
            squares[i] = squares[i] + jnp.sum(gated * gated, axis=1, keepdims=True)
        return squares

    near_at = {0: 0, 1: 1, 2: 2, 8: 3}
    rest_at = {6: 0, 7: 1}
    for i, item in enumerate(ORDER):
        got4(item)
        got1(item)
        if i:
            got3(ORDER[i - 1])
        if i < 3:
            send_own(ORDER[6 + i : 7 + i])
        if i in near_at:
            attend(near_at[i], near, True)
        if i in rest_at:
            got2((KV, rest_at[i]))
            attend(rest_at[i], rest, False)
    got3(ORDER[-1])
    got2((CR, 0))
    rows8 = lax.broadcasted_iota(jnp.int32, (8, 128), 0)
    carries = jnp.where(rows8 == 0, cbuf[0], jnp.where(rows8 == 1, cbuf[1], cbuf[2]))
    enter1[...] = widen(carries)
    z_copy.wait()
    squares = [jnp.zeros((BLK, 1), F32)] * 2
    for quarter in (0, 1):
        got2((ST, quarter))
        squares = finish_ssm(quarter, squares)
    got2((KV, 2))
    attend(2, rest, False)
    for quarter in (2, 3):
        got2((ST, quarter))
        squares = finish_ssm(quarter, squares)
    for i in range(2):
        sq_own[i * BLK : (i + 1) * BLK] = jnp.broadcast_to(squares[i], (BLK, 128))
    sq_copy = pltpu.make_async_remote_copy(
        sq_own, sq_other, qsem.at[0], qsem.at[1], device_id=other, device_id_type=MESH
    )
    got2((KV, 3))
    sq_copy.start()
    attend(3, rest, False)
    sq_copy.wait()
    for i in range(2):
        rows = slice(i * BLK, (i + 1) * BLK)
        total = (sq_own[rows] + sq_other[rows])[:, 0:1]
        norm = lax.rsqrt(total / CHANNELS + EPS)
        ssm_out[rows] = (intra[rows] * norm * gain_ref[...]).astype(BF16)
    for dist in (1, 2, 3, 4):
        for item in ORDER:
            for copy in send(item, 0, dist, at(4)):
                copy.wait_send()


def per_device(
    ssm_input, gate_input, b_input, c_input, step_size, decay_log, skip_gain, norm_gain, queries, key_rows,
    value_rows, doc_lengths,
):
    vm = pl.BlockSpec(memory_space=pltpu.VMEM)
    hbm = pl.BlockSpec(memory_space=pl.ANY)
    sm = pl.BlockSpec(memory_space=pltpu.SMEM)
    dma = pltpu.SemaphoreType.DMA
    skip = skip_gain.reshape(1, 32)
    return pl.pallas_call(
        body,
        out_shape=(
            pltpu.VMEM((ROWS, LANES), BF16),
            pltpu.VMEM((ROWS, 4096), BF16),
        ),
        in_specs=[sm, hbm] + [vm] * 8 + [hbm] * 2,
        out_specs=(vm, vm),
        scratch_shapes=[
            pltpu.VMEM((ROWS, LANES), BF16),
            pltpu.VMEM((ROWS, LANES), BF16),
            pltpu.VMEM((ROWS, 4096), BF16),
            pltpu.VMEM((4, ROWS, 512), BF16),
            pltpu.VMEM((4, ROWS, 512), BF16),
            pltpu.VMEM((4, BLK, LANES), BF16),
            pltpu.VMEM((4, 8, 128), F32),
            pltpu.VMEM((BLK, LANES), BF16),
            pltpu.VMEM((8, 128), F32),
            pltpu.VMEM((ROWS, 128), BF16),
            pltpu.VMEM((5, ROWS, 128), BF16),
            pltpu.VMEM((32, ROWS, 256), F32),
            pltpu.VMEM((32, ROWS, 128), F32),
            pltpu.VMEM((128, ROWS), F32),
            pltpu.VMEM((128, ROWS), F32),
            pltpu.VMEM((8, 128), F32),
            pltpu.VMEM((ROWS, 128), BF16),
            pltpu.VMEM((2, 128, 128), F32),
            pltpu.VMEM((2, 128, 128), F32),
            pltpu.VMEM((2, 128, 128), F32),
            pltpu.VMEM((4, 128, 128), F32),
            pltpu.VMEM((4, 128, 128), F32),
            pltpu.VMEM((ROWS, LANES), F32),
            pltpu.VMEM((ROWS, LANES), F32),
            pltpu.VMEM((BLK, LANES), BF16),
            pltpu.VMEM((BLK, LANES), F32),
            pltpu.VMEM((8, LANES), F32),
            pltpu.VMEM((8, LANES), F32),
            pltpu.VMEM((ROWS, 128), F32),
            pltpu.VMEM((ROWS, 128), F32),
            dma((3,)),
            dma((4, 4, 2)),
            dma((4, 4, 2)),
            dma((4, 5, 2)),
            dma((4, 5, 2)),
            dma((2,)),
        ],
        compiler_params=pltpu.CompilerParams(collective_id=0, has_side_effects=True),
        name="layer",
    )(
        doc_lengths, ssm_input, b_input, c_input, step_size.T, decay_log.T, skip, norm_gain.reshape(1, LANES),
        key_rows, value_rows, gate_input, queries,
    )


def solution(mesh):
    both = P("ctx", "head")
    placed = (both,) * 6 + (P("head"),) * 2 + (both,) * 3 + (P(),)
    return jax.shard_map(
        per_device, mesh=mesh, in_specs=placed, out_specs=(both, both), check_vma=False
    )
```
